32 devices in a mesh: net: 2 (over y), obs: 4 (over z), state: 4 (over x, core).
Axes of the slice: x: 2, y: 2, z: 4, core: 2. Of those that a mesh axis runs over, the one named last changes fastest.
Arguments:
- anomalies: bfloat16 [4, 512, 512], P('state', 'obs'), may hold values from -6 to 6
- prior_ensemble_mean: float32 [4, 512], P('state', 'obs'), may hold values from -6 to 6
- operator_blocks: bfloat16 [64, 4, 8, 128, 128], P(('net', 'obs'), 'state'), parts along dimension 0, may hold values from -0.09375 to 0.09375
- block_column_ids: int32 [64, 4, 8], P(('net', 'obs'), 'state'), parts along dimension 0, may hold values from 0 to 3
- observation_counts: int32 [64], P(('net', 'obs')), parts along dimension 0, may hold values from 1 to 128, as said below
- observed_readings: float32 [64, 128], P(('net', 'obs')), parts along dimension 0, may hold values from -6 to 6
- observation_error_std: float32 [64, 128], P(('net', 'obs')), parts along dimension 0, may hold values from 0.25 to 4
Outputs:
- analysis: bfloat16 [8, 512, 512], P(('net', 'state'), 'obs'), parts along dimension 0
The draws below stay inside these ranges and needn't reach their ends.
There are 2 independent parts, one for each index of `net`. The reference program is written for one: setup_inputs(seed, part) draws one part's arguments, and reference() takes and returns one part's arrays. A program takes and returns all parts, laid end to end along the dimension named above; an argument that names none is the same for every part. Nothing has to cross between parts.
Inputs may be any that keep to these rules, and one draw needn't show every extreme that they name: `observation_counts`: some observation block of every network is full.
All inputs are finite; a program needn't handle non-finite values.
Results may differ from the reference program's by a relative error of at most 0.0053.
Values may be sent and summed in bfloat16 or wider, within the bound.
A program may use at most 64 MiB of HBM per device.

```python
import math
import jax
import jax.numpy as jnp
from jax import lax

MEMBERS = 512
BLOCK_SIZE = 128
NB = 8
STATE_SLAB_COUNT = 4
SLAB_CELL_COUNT = 512
SLAB_BLOCK_COUNT = 4
OBLKS = 32


def draw_observation_counts(key, part):
    first, second = jax.random.split(jax.random.fold_in(key, 11))
    counts = jax.random.randint(first, (OBLKS,), 1, BLOCK_SIZE + 1)
    full_at = jax.random.randint(second, (), 0, OBLKS)
    return jnp.where(jnp.arange(OBLKS) == full_at, BLOCK_SIZE, counts).astype(jnp.int32)


def set_ends(drawn, own_key, smallest, high):
    index_at = [jax.random.randint(jax.random.fold_in(own_key, axis), (), 0, length) for axis, length in enumerate(drawn.shape)]
    longest = drawn.shape.index(max(drawn.shape))
    next_to = index_at[:longest] + [(index_at[longest] + 1) % drawn.shape[longest]] + index_at[longest + 1:]
    return drawn.at[tuple(index_at)].set(smallest).at[tuple(next_to)].set(high)


def level_of(stream_key, shape, cuts, smallest, top_value):
    loudness, own = 1.0, jax.random.fold_in(stream_key, 6)
    for axis_at, parts in cuts:
        heights = jnp.exp(jax.random.uniform(jax.random.fold_in(own, axis_at), (parts,), jnp.float32, smallest / len(cuts), top_value / len(cuts)))
        loudness = loudness * jnp.repeat(heights, shape[axis_at] // parts).reshape([-1 if axis == axis_at else 1 for axis in range(len(shape))])
    return loudness


def bell_draw(key, shape, width, limit, pieces=(), kind=jnp.bfloat16):
    entries = jax.random.normal(key, shape, jnp.float32) * width
    if len(pieces) > 0:
        entries = level_of(key, shape, pieces, -0.22, 0.18) * entries
    return jnp.clip(entries, min=-limit, max=limit).astype(kind)


def setup_inputs(seed: int = 0, part: int = 0) -> dict:
    key_list = jax.random.split(jax.random.key(seed), 8)
    part_keys = jax.random.split(jax.random.fold_in(key_list[7], part), 8)
    anomalies = bell_draw(key_list[0], (STATE_SLAB_COUNT, SLAB_CELL_COUNT, MEMBERS), 1.0, 6.0, ((0, 4), (1, 4)))
    prior_ensemble_mean = bell_draw(key_list[1], (STATE_SLAB_COUNT, SLAB_CELL_COUNT), 1.0, 6.0, ((0, 4), (1, 4)), jnp.float32)
    operator_blocks = bell_draw(part_keys[2], (OBLKS, STATE_SLAB_COUNT, NB, BLOCK_SIZE, BLOCK_SIZE), (STATE_SLAB_COUNT * NB * BLOCK_SIZE) ** -0.5, 0.09375, ((0, 4), (1, 4)))
    block_column_ids = set_ends(jax.random.randint(part_keys[3], (OBLKS, STATE_SLAB_COUNT, NB), 0, SLAB_BLOCK_COUNT), jax.random.fold_in(part_keys[3], 1), 0, SLAB_BLOCK_COUNT - 1).astype(jnp.int32)
    observation_counts = draw_observation_counts(jax.random.fold_in(jax.random.fold_in(key_list[7], part), 71), part)
    observed_readings = jnp.clip(jax.random.uniform(part_keys[5], (OBLKS, BLOCK_SIZE), jnp.float32, -6.0, 6.0) * level_of(part_keys[5], (OBLKS, BLOCK_SIZE), ((0, 4),), -0.4, 0.0), -6.0, 6.0)
    observation_error_std = jnp.clip(jnp.exp(math.log(4.0) - 2.7725887 * jax.random.uniform(part_keys[6], (OBLKS, BLOCK_SIZE), jnp.float32) ** level_of(part_keys[6], (OBLKS, BLOCK_SIZE), ((0, 4),), -0.2, 0.2)), 0.25, 4.0)
    return dict(anomalies=anomalies, prior_ensemble_mean=prior_ensemble_mean, operator_blocks=operator_blocks, block_column_ids=block_column_ids, observation_counts=observation_counts, observed_readings=observed_readings, observation_error_std=observation_error_std)


def reference(anomalies, prior_ensemble_mean, operator_blocks, block_column_ids, observation_counts, observed_readings, observation_error_std):
    members = anomalies.shape[2]
    cells = anomalies.reshape(STATE_SLAB_COUNT, SLAB_BLOCK_COUNT, BLOCK_SIZE, members)
    reduced_mean = prior_ensemble_mean.astype(jnp.bfloat16).reshape(STATE_SLAB_COUNT, SLAB_BLOCK_COUNT, BLOCK_SIZE)
    slab_ids = jnp.arange(STATE_SLAB_COUNT, dtype=jnp.int32)[:, None]

    def one_block(inputs):
        values, columns = inputs
        picked = cells[slab_ids, columns]
        picked_mean = reduced_mean[slab_ids, columns]
        wide = values.astype(jnp.float32)
        rows_anom = jnp.einsum('sjrc,sjck->rk', wide, picked.astype(jnp.float32))
        rows_mean = jnp.einsum('sjrc,sjc->r', wide, picked_mean.astype(jnp.float32))
        return (rows_anom, rows_mean)
    obs_anom, obs_mean = lax.map(one_block, (operator_blocks, block_column_ids))
    obs_anom = obs_anom.reshape(OBLKS * BLOCK_SIZE, members)
    obs_mean = obs_mean.reshape(OBLKS * BLOCK_SIZE)
    valid = (jnp.arange(BLOCK_SIZE, dtype=jnp.int32)[None, :] < observation_counts[:, None]).astype(jnp.float32)
    weight = (valid / observation_error_std).reshape(OBLKS * BLOCK_SIZE)
    scaled = obs_anom * weight[:, None]
    innovation = weight * (observed_readings.reshape(OBLKS * BLOCK_SIZE) - obs_mean)
    gram = jnp.dot(scaled.T, scaled, precision=lax.Precision.HIGHEST)
    gram = gram + (members - 1.0) * jnp.eye(members, dtype=jnp.float32)
    rhs = jnp.dot(scaled.T, innovation[:, None], precision=lax.Precision.HIGHEST)
    lower = jnp.linalg.cholesky(gram)
    middle = lax.linalg.triangular_solve(lower, rhs, left_side=True, lower=True)
    mean_weights = lax.linalg.triangular_solve(lower, middle, left_side=True, lower=True, transpose_a=True)
    identity = jnp.eye(members, dtype=jnp.float32)
    transform = jnp.sqrt(members - 1.0) * lax.linalg.triangular_solve(lower, identity, left_side=True, lower=True, transpose_a=True)
    mixing = (transform + mean_weights).astype(jnp.bfloat16)
    flat = anomalies.reshape(STATE_SLAB_COUNT * SLAB_CELL_COUNT, members)
    shifted_values = jnp.dot(flat.astype(jnp.float32), mixing.astype(jnp.float32), preferred_element_type=jnp.float32)
    analysis_output = prior_ensemble_mean.reshape(STATE_SLAB_COUNT * SLAB_CELL_COUNT)[:, None] + shifted_values
    return analysis_output.astype(jnp.bfloat16).reshape(STATE_SLAB_COUNT, SLAB_CELL_COUNT, members)
```

```python
import functools
import jax
import jax.numpy as jnp
from jax import lax
from jax.experimental import pallas as pl
from jax.experimental.pallas import tpu as pltpu
from jax.sharding import PartitionSpec as P

BLK = 128
HI = lax.Precision.HIGHEST
NT = (((1,), (1,)), ((), ()))


def inverse_factor(block):
    row = lax.broadcasted_iota(jnp.int32, (BLK, BLK), 0)
    col = lax.broadcasted_iota(jnp.int32, (BLK, BLK), 1)
    eye = (row == col).astype(jnp.float32)
    groups = BLK // 8
    left = [block[8 * g : 8 * g + 8] for g in range(groups)]
    right = [eye[8 * g : 8 * g + 8] for g in range(groups)]
    sub = lax.broadcasted_iota(jnp.int32, (8, 1), 0)
    for k in range(BLK - 1):
        g, i = divmod(k, 8)
        lrow = left[g][i : i + 1, :]
        rrow = right[g][i : i + 1, :]
        inv = 1.0 / lrow[:, k : k + 1]
        lrow = lrow * inv
        rrow = rrow * inv
        for h in range(g, groups):
            c = left[h][:, k : k + 1]
            if h == g:
                if i == 7:
                    continue
                c = jnp.where(sub > i, c, 0.0)
            left[h] = left[h] - c * lrow
            right[h] = right[h] - c * rrow
    full = jnp.concatenate(left, axis=0)
    diag = jnp.sum(jnp.where(row == col, full, 0.0), axis=1, keepdims=True)
    return jnp.concatenate(right, axis=0) * lax.rsqrt(diag)


def finish_kernel(gram_ref, rhs_ref, anom_ref, mean_ref, out_ref, work):
    members = gram_ref.shape[1]
    cells = anom_ref.shape[0]
    total = members + cells + 8
    work[0:members, :] = gram_ref[...]
    work[members : members + cells, :] = anom_ref[...].astype(jnp.float32)
    work[members + cells : total, :] = rhs_ref[...]

    @pl.loop(0, members // BLK)
    def _(p):
        off = pl.multiple_of(p * BLK, BLK)
        inv = inverse_factor(work[pl.ds(off, BLK), pl.ds(off, BLK)])
        x = lax.dot_general(
            work[:, pl.ds(off, BLK)], inv, NT, precision=HI, preferred_element_type=jnp.float32
        )
        rows = lax.broadcasted_iota(jnp.int32, (total, 1), 0)
        x = jnp.where(rows >= off + BLK, x, 0.0)
        work[...] -= lax.dot_general(
            x, x[:members], NT, precision=HI, preferred_element_type=jnp.float32
        )
        work[members:total, pl.ds(off, BLK)] = x[members:]

    solved = work[members : members + cells, :]
    shift = jnp.sum(solved * work[members + cells : members + cells + 1, :], axis=1, keepdims=True)
    root = (members - 1.0) ** 0.5
    out_ref[...] = (mean_ref[...] + (root * solved + shift)).astype(jnp.bfloat16)


def finish(gram, rhs_rows, cells, mean_col):
    members = gram.shape[1]
    ncells = cells.shape[0]
    return pl.pallas_call(
        finish_kernel,
        out_shape=jax.ShapeDtypeStruct((ncells, members), jnp.bfloat16),
        in_specs=[pl.BlockSpec(memory_space=pltpu.VMEM)] * 4,
        out_specs=pl.BlockSpec(memory_space=pltpu.VMEM),
        scratch_shapes=[pltpu.VMEM((members + ncells + 8, members), jnp.float32)],
        compiler_params=pltpu.CompilerParams(vmem_limit_bytes=32 << 20),
    )(gram, rhs_rows, cells, mean_col)


def local(
    anomalies,
    prior_ensemble_mean,
    operator_blocks,
    block_column_ids,
    observation_counts,
    observed_readings,
    observation_error_std,
):
    members = anomalies.shape[2]
    blk = operator_blocks.shape[3]
    local_cells = anomalies[0]
    slab_local_mean = prior_ensemble_mean[0]
    slab_anom, slab_mean = (
        lax.all_gather(local_cells, "obs", axis=0, tiled=True),
        lax.all_gather(slab_local_mean.astype(jnp.bfloat16), "obs", axis=0, tiled=True),
    )
    nblocks = slab_anom.shape[0] // blk
    cells = slab_anom.reshape(nblocks, blk, members)
    mean_blocks = slab_mean.reshape(nblocks, blk)

    def one_block(inputs):
        values, columns = inputs
        picked = cells[columns]
        picked_mean = mean_blocks[columns]
        rows_anom = jnp.einsum("jrc,jck->rk", values, picked, preferred_element_type=jnp.float32)
        rows_mean = jnp.einsum("jrc,jc->r", values, picked_mean, preferred_element_type=jnp.float32)
        return (rows_anom, rows_mean)

    part_anom, part_mean = lax.map(one_block, (operator_blocks[:, 0], block_column_ids[:, 0]))
    nrows = part_anom.shape[0] * blk
    part_anom = part_anom.reshape(nrows, members)
    part_mean = part_mean.reshape(nrows)
    valid = (jnp.arange(blk, dtype=jnp.int32)[None, :] < observation_counts[:, None]).astype(
        jnp.float32
    )
    weight_all = (valid / observation_error_std).reshape(nrows)
    observed_all = observed_readings.reshape(nrows)
    obs_anom, obs_mean = lax.psum((part_anom, part_mean), "state")
    scaled = obs_anom * weight_all[:, None]
    innovation = weight_all * (observed_all - obs_mean)
    gram_part = jnp.dot(scaled.T, scaled, precision=lax.Precision.HIGHEST)
    rhs_part = jnp.dot(scaled.T, innovation[:, None], precision=lax.Precision.HIGHEST)
    gram, rhs = lax.psum((gram_part, rhs_part), "obs")
    identity = jnp.eye(members, dtype=jnp.float32)
    gram = gram + (members - 1.0) * identity
    rhs_rows = jnp.concatenate([rhs.T, jnp.zeros((7, members), jnp.float32)], axis=0)
    out = finish(gram, rhs_rows, local_cells, slab_local_mean[:, None])
    return out[None]


def solution(mesh):
    placed = (
        P("state", "obs", None),
        P("state", "obs"),
        P(("net", "obs"), "state", None, None, None),
        P(("net", "obs"), "state", None),
        P(("net", "obs")),
        P(("net", "obs"), None),
        P(("net", "obs"), None),
    )
    return jax.shard_map(
        local,
        mesh=mesh,
        in_specs=placed,
        out_specs=P(("net", "state"), "obs", None),
        check_vma=False,
    )
```

```python
import functools
import jax
import jax.numpy as jnp
from jax import lax
from jax.experimental import pallas as pl
from jax.experimental.pallas import tpu as pltpu
from jax.sharding import PartitionSpec as P

BLK = 128
HI = lax.Precision.HIGHEST
NT = (((1,), (1,)), ((), ()))


def inverse_factor(block):
    row = lax.broadcasted_iota(jnp.int32, (BLK, BLK), 0)
    col = lax.broadcasted_iota(jnp.int32, (BLK, BLK), 1)
    eye = (row == col).astype(jnp.float32)
    groups = BLK // 8
    left = [block[8 * g : 8 * g + 8] for g in range(groups)]
    right = [eye[8 * g : 8 * g + 8] for g in range(groups)]
    sub = lax.broadcasted_iota(jnp.int32, (8, 1), 0)
    for k in range(BLK - 1):
        g, i = divmod(k, 8)
        lrow = left[g][i : i + 1, :]
        rrow = right[g][i : i + 1, :]
        inv = 1.0 / lrow[:, k : k + 1]
        lrow = lrow * inv
        rrow = rrow * inv
        for h in range(g, groups):
            c = left[h][:, k : k + 1]
            if h == g:
                if i == 7:
                    continue
                c = jnp.where(sub > i, c, 0.0)
            left[h] = left[h] - c * lrow
            right[h] = right[h] - c * rrow
    full = jnp.concatenate(left, axis=0)
    diag = jnp.sum(jnp.where(row == col, full, 0.0), axis=1, keepdims=True)
    return jnp.concatenate(right, axis=0) * lax.rsqrt(diag)


def finish_kernel(packed_ref, anom_ref, mean_ref, out_ref, work):
    cells, members = anom_ref.shape
    total = members + cells + 8
    row = lax.broadcasted_iota(jnp.int32, (BLK, BLK), 0)
    col = lax.broadcasted_iota(jnp.int32, (BLK, BLK), 1)
    ridge = jnp.where(row == col, members - 1.0, 0.0)
    start = 0
    for j in range(members // BLK):
        size = members - j * BLK
        cols = slice(j * BLK, (j + 1) * BLK)
        if j:
            work[0 : j * BLK, cols] = jnp.zeros((j * BLK, BLK), jnp.float32)
        work[cols, cols] = packed_ref[start : start + BLK, :] + ridge
        if size > BLK:
            work[(j + 1) * BLK : members, cols] = packed_ref[start + BLK : start + size, :]
        start += size
    for j in range(members // BLK):
        cols = slice(j * BLK, (j + 1) * BLK)
        work[members + cells : total, cols] = jnp.broadcast_to(
            packed_ref[start + j : start + j + 1, :], (8, BLK)
        )
    work[members : members + cells, :] = anom_ref[...].astype(jnp.float32)

    @pl.loop(0, members // BLK)
    def _(p):
        off = pl.multiple_of(p * BLK, BLK)
        inv = inverse_factor(work[pl.ds(off, BLK), pl.ds(off, BLK)])
        x = lax.dot_general(
            work[:, pl.ds(off, BLK)], inv, NT, precision=HI, preferred_element_type=jnp.float32
        )
        rows = lax.broadcasted_iota(jnp.int32, (total, 1), 0)
        x = jnp.where(rows >= off + BLK, x, 0.0)
        work[...] -= lax.dot_general(
            x, x[:members], NT, precision=HI, preferred_element_type=jnp.float32
        )
        work[members:total, pl.ds(off, BLK)] = x[members:]

    solved = work[members : members + cells, :]
    shift = jnp.sum(solved * work[members + cells : members + cells + 1, :], axis=1, keepdims=True)
    root = (members - 1.0) ** 0.5
    out_ref[...] = (mean_ref[...] + (root * solved + shift)).astype(jnp.bfloat16)


def finish(packed, cells, mean_col):
    ncells, members = cells.shape
    return pl.pallas_call(
        finish_kernel,
        out_shape=jax.ShapeDtypeStruct((ncells, members), jnp.bfloat16),
        in_specs=[pl.BlockSpec(memory_space=pltpu.VMEM)] * 3,
        out_specs=pl.BlockSpec(memory_space=pltpu.VMEM),
        scratch_shapes=[pltpu.VMEM((members + ncells + 8, members), jnp.float32)],
        compiler_params=pltpu.CompilerParams(vmem_limit_bytes=32 << 20),
    )(packed, cells, mean_col)


def packed_rows(members, ways):
    need = 8
    for j in range(members // BLK):
        need += members - j * BLK
    step = 8 * ways
    return (need + step - 1) // step * step


def bits_of(n):
    return [1 << t for t in range(n.bit_length() - 1)]


def observe_kernel(
    obs_n, state_n, ids_ref, counts_ref, cells_ref, mean_ref, ops_ref, read_ref, std_ref, out_ref,
    slab, slab_mean, part, sent, got, inno, inno_got, acc, acc_got, full,
    right_send, right_recv, left_send, left_recv, part_send, part_recv, acc_send, acc_recv,
):
    me_o, me_s = lax.axis_index("obs"), lax.axis_index("state")
    nb, slots = ops_ref.shape[0], ops_ref.shape[1]
    members = cells_ref.shape[1]
    state_bits, obs_bits = bits_of(state_n), bits_of(obs_n)

    def partner(axis, bit):
        me = me_s if axis == "state" else me_o
        return me + bit - 2 * bit * ((me // bit) % 2)

    slab[me_o] = cells_ref[...]
    slab_mean[me_o] = jnp.broadcast_to(mean_ref[...], (16, BLK)).astype(jnp.bfloat16)

    barrier = pltpu.get_barrier_semaphore()
    greeted = [{"obs": lax.rem(me_o + 1, obs_n)}, {"obs": lax.rem(me_o + obs_n - 1, obs_n)}]
    greeted += [{"obs": partner("obs", b)} for b in obs_bits]
    greeted += [{"state": partner("state", b)} for b in state_bits]
    for where in greeted:
        pl.semaphore_signal(barrier, inc=1, device_id=where, device_id_type=pl.DeviceIdType.MESH)
    pl.semaphore_wait(barrier, len(greeted))

    def remote(src, dst, send, recv, where):
        return pltpu.make_async_remote_copy(
            src_ref=src, dst_ref=dst, send_sem=send, recv_sem=recv,
            device_id=where, device_id_type=pl.DeviceIdType.MESH,
        )

    def hop(block, sends, recvs, t, to):
        return [
            remote(slab.at[block], slab.at[block], sends.at[0, t], recvs.at[0, t], {"obs": to}),
            remote(slab_mean.at[block], slab_mean.at[block], sends.at[1, t], recvs.at[1, t], {"obs": to}),
        ]

    def clip(x):
        return jnp.clip(x, 0, obs_n - 1)

    for t in range(obs_n - 1):
        @pl.when((me_o < obs_n - 1) & (me_o - t >= 0))
        def _():
            for c in hop(clip(me_o - t), right_send, right_recv, t, clip(me_o + 1)):
                c.start()

        @pl.when((me_o > 0) & (me_o + t <= obs_n - 1))
        def _():
            for c in hop(clip(me_o + t), left_send, left_recv, t, clip(me_o - 1)):
                c.start()

        @pl.when(me_o - 1 - t >= 0)
        def _():
            for c in hop(clip(me_o - 1 - t), right_send, right_recv, t, clip(me_o - 1)):
                c.wait_recv()

        @pl.when(me_o + 1 + t <= obs_n - 1)
        def _():
            for c in hop(clip(me_o + 1 + t), left_send, left_recv, t, clip(me_o + 1)):
                c.wait_recv()

    lane = lax.broadcasted_iota(jnp.int32, (1, BLK), 1)

    def observe(b):
        rows = jnp.zeros((BLK, members), jnp.float32)
        mean = jnp.zeros((16, BLK), jnp.float32)
        for j in range(slots):
            column = ids_ref[b, j]
            op = ops_ref[b, j]
            rows += jnp.dot(op, slab[column], preferred_element_type=jnp.float32)
            mean += lax.dot_general(slab_mean[column], op, NT, preferred_element_type=jnp.float32)
        weight = jnp.where(lane < counts_ref[b], 1.0 / std_ref[pl.ds(b, 1), :], 0.0)
        inno[pl.ds(b, 1), :] = weight * (read_ref[pl.ds(b, 1), :] * (1.0 / state_n) - mean[0:1])
        return rows * jnp.broadcast_to(weight, (BLK, BLK)).T[:, 0:1]

    half = nb // 2
    low = 0
    for t, bit in enumerate(state_bits):
        high_bit = (me_s // bit) % 2
        keep = high_bit * half
        give = half - keep
        if t == 0:
            @pl.loop(0, half)
            def _(i):
                sent[i] = observe(give + i).astype(jnp.bfloat16)
        else:
            sent[0:half] = part[pl.ds(low + give, half)].astype(jnp.bfloat16)
        off = 0 if t == 0 else nb - 2 * half
        where = {"state": partner("state", bit)}
        copy = remote(
            sent.at[pl.ds(0, half)], got.at[pl.ds(off, half)], part_send.at[0, t], part_recv.at[0, t], where
        )
        copy.start()
        if t == 0:
            @pl.loop(0, half)
            def _(i):
                part[keep + i] = observe(keep + i)
        small = remote(inno, inno_got.at[t], part_send.at[1, t], part_recv.at[1, t], where)
        small.start()
        copy.wait()
        small.wait()
        low = low + keep
        part[pl.ds(low, half)] += got[off : off + half].astype(jnp.float32)
        inno[...] += inno_got[t]
        half //= 2
    own = nb // state_n

    scaled = part[pl.ds(low, own)].reshape(own * BLK, members)
    row = 0
    for j in range(members // BLK):
        size = members - j * BLK
        acc[row : row + size, :] = lax.dot_general(
            scaled[:, j * BLK :], scaled[:, j * BLK : (j + 1) * BLK], (((0,), (0,)), ((), ())),
            precision=HI, preferred_element_type=jnp.float32,
        )
        row += size
    rhs = jnp.zeros((8, members), jnp.float32)
    for i in range(own):
        rhs += jnp.dot(
            jnp.broadcast_to(inno[pl.ds(low + i, 1), :], (8, BLK)), scaled[i * BLK : (i + 1) * BLK],
            precision=HI, preferred_element_type=jnp.float32,
        )
    acc[row:, :] = jnp.zeros((acc.shape[0] - row, BLK), jnp.float32)
    for j in range(members // BLK):
        acc[row + j : row + j + 1, :] = rhs[0:1, j * BLK : (j + 1) * BLK]

    steps = [("state", b) for b in state_bits] + [("obs", b) for b in obs_bits]
    size = acc.shape[0]
    base = 0
    spot = 0
    trail = []
    for n, (axis, bit) in enumerate(steps):
        size //= 2
        keep = ((me_s if axis == "state" else me_o) // bit) % 2 * size
        where = {axis: partner(axis, bit)}
        give = pl.multiple_of(base + size - keep, 8)
        copy = remote(
            acc.at[pl.ds(give, size)], acc_got.at[pl.ds(spot, size)], acc_send.at[n], acc_recv.at[n], where
        )
        copy.start()
        copy.wait()
        base = pl.multiple_of(base + keep, 8)
        acc[pl.ds(base, size), :] += acc_got[spot : spot + size, :]
        spot += size
        trail.append((n, where, base, size))
    full[pl.ds(base, size), :] = acc[pl.ds(base, size), :]
    for n, where, base, size in reversed(trail):
        m = len(steps) + n
        copy = remote(
            full.at[pl.ds(base, size)], full.at[pl.ds(base, size)], acc_send.at[m], acc_recv.at[m], where
        )
        copy.start()
        copy.wait()

    for t in range(obs_n - 1):
        @pl.when((me_o < obs_n - 1) & (me_o - t >= 0))
        def _():
            for c in hop(clip(me_o - t), right_send, right_recv, t, clip(me_o + 1)):
                c.wait_send()

        @pl.when((me_o > 0) & (me_o + t <= obs_n - 1))
        def _():
            for c in hop(clip(me_o + t), left_send, left_recv, t, clip(me_o - 1)):
                c.wait_send()
    out_ref[...] = full[...]


def observe(obs_n, state_n, ids, counts, cells, mean_row, ops, readings, stds):
    nb = ops.shape[0]
    members = cells.shape[1]
    rows = packed_rows(members, obs_n * state_n)
    nsteps = 2 * (len(bits_of(obs_n)) + len(bits_of(state_n)))
    hops = pltpu.SemaphoreType.DMA((2, obs_n - 1))
    pieces = pltpu.SemaphoreType.DMA((2, len(bits_of(state_n))))
    return pl.pallas_call(
        functools.partial(observe_kernel, obs_n, state_n),
        out_shape=jax.ShapeDtypeStruct((rows, BLK), jnp.float32),
        in_specs=[pl.BlockSpec(memory_space=pltpu.SMEM)] * 2
        + [pl.BlockSpec(memory_space=pltpu.VMEM)] * 5,
        out_specs=pl.BlockSpec(memory_space=pltpu.VMEM),
        scratch_shapes=[
            pltpu.VMEM((obs_n, BLK, members), jnp.bfloat16),
            pltpu.VMEM((obs_n, 16, BLK), jnp.bfloat16),
            pltpu.VMEM((nb, BLK, members), jnp.float32),
            pltpu.VMEM((nb // 2, BLK, members), jnp.bfloat16),
            pltpu.VMEM((nb, BLK, members), jnp.bfloat16),
            pltpu.VMEM((nb, BLK), jnp.float32),
            pltpu.VMEM((len(bits_of(state_n)), nb, BLK), jnp.float32),
            pltpu.VMEM((rows, BLK), jnp.float32),
            pltpu.VMEM((rows, BLK), jnp.float32),
            pltpu.VMEM((rows, BLK), jnp.float32),
            hops, hops, hops, hops, pieces, pieces,
            pltpu.SemaphoreType.DMA((nsteps,)),
            pltpu.SemaphoreType.DMA((nsteps,)),
        ],
        compiler_params=pltpu.CompilerParams(
            collective_id=0, has_side_effects=True, vmem_limit_bytes=48 << 20
        ),
    )(ids, counts, cells, mean_row, ops, readings, stds)


def local(
    obs_n,
    state_n,
    anomalies,
    prior_ensemble_mean,
    operator_blocks,
    block_column_ids,
    observation_counts,
    observed_readings,
    observation_error_std,
):
    cells = anomalies[0]
    packed = observe(
        obs_n, state_n, block_column_ids[:, 0], observation_counts, cells, prior_ensemble_mean,
        operator_blocks[:, 0], observed_readings, observation_error_std,
    )
    return finish(packed, cells, prior_ensemble_mean.reshape(-1, 1))[None]


def solution(mesh):
    placed = (
        P("state", "obs", None),
        P("state", "obs"),
        P(("net", "obs"), "state", None, None, None),
        P(("net", "obs"), "state", None),
        P(("net", "obs")),
        P(("net", "obs"), None),
        P(("net", "obs"), None),
    )
    return jax.shard_map(
        functools.partial(local, mesh.shape["obs"], mesh.shape["state"]),
        mesh=mesh,
        in_specs=placed,
        out_specs=P(("net", "state"), "obs", None),
        check_vma=False,
    )
```

```python
import functools
import jax
import jax.numpy as jnp
from jax import lax
from jax.experimental import pallas as pl
from jax.experimental.pallas import tpu as pltpu
from jax.sharding import PartitionSpec as P

BLK = 128
HI = lax.Precision.HIGHEST
NT = (((1,), (1,)), ((), ()))


def inverse_factor(block, width=32):
    row = lax.broadcasted_iota(jnp.int32, (BLK, BLK), 0)
    col = lax.broadcasted_iota(jnp.int32, (BLK, BLK), 1)
    eye = (row == col).astype(jnp.float32)
    groups = BLK // 8
    left = [block[8 * g : 8 * g + 8] for g in range(groups)]
    right = [eye[8 * g : 8 * g + 8] for g in range(groups)]
    sub = lax.broadcasted_iota(jnp.int32, (8, 1), 0)
    lane = lax.broadcasted_iota(jnp.int32, (1, BLK), 1)
    local = width // 8
    for start in range(0, BLK, width):
        g0 = start // 8
        spread = [
            [jnp.broadcast_to(left[g0 + h][:, start + j : start + j + 1], (8, BLK)) for h in range(local)]
            for j in range(width)
        ]
        scaled = []
        roots = []
        for j in range(width):
            gj, ij = divmod(j, 8)
            pivot = spread[j][gj][ij : ij + 1]
            inv = 1.0 / pivot
            lrow = left[g0 + gj][ij : ij + 1] * inv
            rrow = right[g0 + gj][ij : ij + 1] * inv
            scaled.append(lrow)
            roots.append(lax.rsqrt(pivot))
            shared = [None if t <= j else spread[t][gj][ij : ij + 1] * inv for t in range(width)]
            for h in range(gj, local):
                m = spread[j][h]
                if h == gj:
                    if ij == 7:
                        continue
                    m = jnp.where(sub > ij, m, 0.0)
                for t in range(j + 1, width):
                    spread[t][h] = spread[t][h] - m * shared[t]
                left[g0 + h] = left[g0 + h] - m * lrow
                right[g0 + h] = right[g0 + h] - m * rrow
        upper_l = jnp.concatenate(left[g0 : g0 + local], axis=0)
        upper_r = jnp.concatenate(right[g0 : g0 + local], axis=0)
        end = start + width
        if end < BLK:
            low = jnp.where(lane >= end, jnp.concatenate(scaled, axis=0), 0.0)
            change = lax.dot_general(
                low, jnp.concatenate([upper_l, upper_r], axis=1), (((0,), (0,)), ((), ())),
                precision=HI, preferred_element_type=jnp.float32,
            )
            for h in range(end // 8, groups):
                left[h] = left[h] - change[8 * h : 8 * h + 8, :BLK]
                right[h] = right[h] - change[8 * h : 8 * h + 8, BLK:]
        scale = jnp.concatenate(roots, axis=0)
        for h in range(local):
            right[g0 + h] = right[g0 + h] * scale[8 * h : 8 * h + 8]
    return jnp.concatenate(right, axis=0)


def finish_kernel(packed_ref, anom_ref, mean_ref, out_ref, work):
    cells, members = anom_ref.shape
    total = members + cells + 8
    row = lax.broadcasted_iota(jnp.int32, (BLK, BLK), 0)
    col = lax.broadcasted_iota(jnp.int32, (BLK, BLK), 1)
    ridge = jnp.where(row == col, members - 1.0, 0.0)
    start = 0
    last = packed_ref.shape[0] - 8
    for j in range(members // BLK):
        size = members - j * BLK
        cols = slice(j * BLK, (j + 1) * BLK)
        if j:
            work[0 : j * BLK, cols] = jnp.zeros((j * BLK, BLK), jnp.float32)
        work[cols, cols] = packed_ref[start : start + BLK, :] + ridge
        if size > BLK:
            work[(j + 1) * BLK : members, cols] = packed_ref[start + BLK : start + size, :]
        start += size
    for j in range(members // BLK):
        cols = slice(j * BLK, (j + 1) * BLK)
        work[members + cells : total, cols] = jnp.broadcast_to(
            packed_ref[last + j : last + j + 1, :], (8, BLK)
        )
    work[members : members + cells, :] = anom_ref[...].astype(jnp.float32)

    @pl.loop(0, members // BLK)
    def _(p):
        off = pl.multiple_of(p * BLK, BLK)
        inv = inverse_factor(work[pl.ds(off, BLK), pl.ds(off, BLK)])
        x = lax.dot_general(
            work[:, pl.ds(off, BLK)], inv, NT, precision=HI, preferred_element_type=jnp.float32
        )
        rows = lax.broadcasted_iota(jnp.int32, (total, 1), 0)
        x = jnp.where(rows >= off + BLK, x, 0.0)
        work[...] -= lax.dot_general(
            x, x[:members], NT, precision=HI, preferred_element_type=jnp.float32
        )
        work[members:total, pl.ds(off, BLK)] = x[members:]

    solved = work[members : members + cells, :]
    shift = jnp.sum(solved * work[members + cells : members + cells + 1, :], axis=1, keepdims=True)
    root = (members - 1.0) ** 0.5
    mean = jnp.broadcast_to(mean_ref[...], (BLK, cells)).T[:, 0:1]
    out_ref[...] = (mean + (root * solved + shift)).astype(jnp.bfloat16)


def finish(packed, cells, mean_row):
    ncells, members = cells.shape
    return pl.pallas_call(
        finish_kernel,
        out_shape=jax.ShapeDtypeStruct((ncells, members), jnp.bfloat16),
        in_specs=[pl.BlockSpec(memory_space=pltpu.VMEM)] * 3,
        out_specs=pl.BlockSpec(memory_space=pltpu.VMEM),
        scratch_shapes=[pltpu.VMEM((members + ncells + 8, members), jnp.float32)],
        compiler_params=pltpu.CompilerParams(vmem_limit_bytes=32 << 20),
    )(packed, cells, mean_row)


def packed_rows(members, ways):
    need = sum(members - j * BLK for j in range(members // BLK))
    step = 16 * ways
    return (need + step - 1) // step * step


def bits_of(n):
    return [1 << t for t in range(n.bit_length() - 1)]


def observe_kernel(
    obs_n, state_n, ids_ref, counts_ref, cells_hbm, mean_hbm, ops_hbm, read_hbm, std_hbm, out_ref,
    mean_row, ops_ref, read_ref, std_ref, load_sem,
    slab, slab_mean, part, sent, got, inno, inno_got, acc, acc_got, full, rhs_sum, rhs_got,
    right_send, right_recv, left_send, left_recv, part_send, part_recv, inno_send, inno_recv,
    acc_send, acc_recv, rhs_send, rhs_recv,
):
    me_o, me_s = lax.axis_index("obs"), lax.axis_index("state")
    nb, slots = ops_ref.shape[0], ops_ref.shape[1]
    members = slab.shape[2]
    state_bits, obs_bits = bits_of(state_n), bits_of(obs_n)

    loads = [
        pltpu.make_async_copy(src, dst, load_sem.at[n])
        for n, (src, dst) in enumerate([
            (cells_hbm, slab.at[me_o]), (mean_hbm, mean_row), (read_hbm, read_ref),
            (std_hbm, std_ref), (ops_hbm, ops_ref),
        ])
    ]
    for load in loads:
        load.start()

    def partner(axis, bit):
        me = me_s if axis == "state" else me_o
        return me + bit - 2 * bit * ((me // bit) % 2)

    barrier = pltpu.get_barrier_semaphore()
    greeted = [{"obs": lax.rem(me_o + 1, obs_n)}, {"obs": lax.rem(me_o + obs_n - 1, obs_n)}]
    greeted += [{"obs": partner("obs", b)} for b in obs_bits]
    greeted += [{"state": partner("state", b)} for b in state_bits]
    for where in greeted:
        pl.semaphore_signal(barrier, inc=1, device_id=where, device_id_type=pl.DeviceIdType.MESH)
    loads[0].wait()
    loads[1].wait()
    slab_mean[me_o] = jnp.broadcast_to(mean_row[...], (16, BLK)).astype(jnp.bfloat16)
    pl.semaphore_wait(barrier, len(greeted))

    def remote(src, dst, send, recv, where):
        return pltpu.make_async_remote_copy(
            src_ref=src, dst_ref=dst, send_sem=send, recv_sem=recv,
            device_id=where, device_id_type=pl.DeviceIdType.MESH,
        )

    def hop(block, sends, recvs, t, to):
        return [
            remote(slab.at[block], slab.at[block], sends.at[0, t], recvs.at[0, t], {"obs": to}),
            remote(slab_mean.at[block], slab_mean.at[block], sends.at[1, t], recvs.at[1, t], {"obs": to}),
        ]

    def clip(x):
        return jnp.clip(x, 0, obs_n - 1)

    for t in range(obs_n - 1):
        @pl.when((me_o < obs_n - 1) & (me_o - t >= 0))
        def _():
            for c in hop(clip(me_o - t), right_send, right_recv, t, clip(me_o + 1)):
                c.start()

        @pl.when((me_o > 0) & (me_o + t <= obs_n - 1))
        def _():
            for c in hop(clip(me_o + t), left_send, left_recv, t, clip(me_o - 1)):
                c.start()

        @pl.when(me_o - 1 - t >= 0)
        def _():
            for c in hop(clip(me_o - 1 - t), right_send, right_recv, t, clip(me_o - 1)):
                c.wait_recv()

        @pl.when(me_o + 1 + t <= obs_n - 1)
        def _():
            for c in hop(clip(me_o + 1 + t), left_send, left_recv, t, clip(me_o + 1)):
                c.wait_recv()

    for load in loads[2:]:
        load.wait()
    lane = lax.broadcasted_iota(jnp.int32, (1, BLK), 1)

    def weight_of(b):
        return jnp.where(lane < counts_ref[b], 1.0 / std_ref[pl.ds(b, 1), :], 0.0)

    @pl.loop(0, nb)
    def _(b):
        mean = jnp.zeros((16, BLK), jnp.float32)
        for j in range(slots):
            mean += lax.dot_general(
                slab_mean[ids_ref[b, j]], ops_ref[b, j], NT, preferred_element_type=jnp.float32
            )
        share = read_ref[pl.ds(b, 1), :] * (1.0 / state_n)
        inno[pl.ds(b, 1), :] = weight_of(b) * (share - mean[0:1])

    def inno_copy(t):
        where = {"state": partner("state", state_bits[t])}
        return remote(inno, inno_got.at[t], inno_send.at[t], inno_recv.at[t], where)

    inno_copy(0).start()

    def observe(b):
        rows = jnp.zeros((BLK, members), jnp.float32)
        for j in range(slots):
            rows += jnp.dot(ops_ref[b, j], slab[ids_ref[b, j]], preferred_element_type=jnp.float32)
        return rows * jnp.broadcast_to(weight_of(b), (BLK, BLK)).T[:, 0:1]

    def part_copy(t, i):
        n = nb - (nb >> t) + i
        where = {"state": partner("state", state_bits[t])}
        return remote(sent.at[n], got.at[n], part_send.at[n], part_recv.at[n], where)

    lows = [0]
    for t, bit in enumerate(state_bits):
        half = nb >> (t + 1)
        keep = (me_s // bit) % 2 * half
        give = lows[-1] + half - keep
        lows.append(lows[-1] + keep)

        def total(b, upto):
            value = observe(b)
            for u in range(upto):
                part_copy(u, b - lows[u + 1]).wait_recv()
                value += got[nb - (nb >> u) + b - lows[u + 1]].astype(jnp.float32)
            return value

        @pl.loop(0, half)
        def _(i):
            sent[nb - (nb >> t) + i] = total(give + i, t).astype(jnp.bfloat16)
            part_copy(t, i).start()

        inno_copy(t).wait()
        inno[...] += inno_got[t]
        if t + 1 < len(state_bits):
            inno_copy(t + 1).start()
    own = nb // state_n
    low = lows[-1]
    last = len(state_bits) - 1

    @pl.loop(0, own)
    def _(i):
        value = observe(low + i)
        for u in range(last):
            part_copy(u, low + i - lows[u + 1]).wait_recv()
            value += got[nb - (nb >> u) + low + i - lows[u + 1]].astype(jnp.float32)
        part[i] = value

    @pl.loop(0, own)
    def _(i):
        part_copy(last, i).wait_recv()
        part[i] += got[nb - (nb >> last) + i].astype(jnp.float32)

    scaled = part[...].reshape(own * BLK, members)
    row = 0
    for j in range(members // BLK):
        size = members - j * BLK
        acc[row : row + size, :] = lax.dot_general(
            scaled[:, j * BLK :], scaled[:, j * BLK : (j + 1) * BLK], (((0,), (0,)), ((), ())),
            precision=HI, preferred_element_type=jnp.float32,
        )
        row += size
    if row < acc.shape[0]:
        acc[row:, :] = jnp.zeros((acc.shape[0] - row, BLK), jnp.float32)
    rhs = jnp.zeros((8, members), jnp.float32)
    for i in range(own):
        rhs += jnp.dot(
            jnp.broadcast_to(inno[pl.ds(low + i, 1), :], (8, BLK)), scaled[i * BLK : (i + 1) * BLK],
            precision=HI, preferred_element_type=jnp.float32,
        )
    rhs_sum[...] = jnp.zeros((8, BLK), jnp.float32)
    for j in range(members // BLK):
        rhs_sum[j : j + 1, :] = rhs[0:1, j * BLK : (j + 1) * BLK]

    by_state = [("state", b) for b in state_bits]
    by_obs = [("obs", b) for b in obs_bits]
    orders = [by_state + by_obs, by_state[:1] + by_obs + by_state[1:]]
    steps = len(orders[0])
    size = acc.shape[0] // 2
    bases = [0, size]
    spots = [0, size]
    trail = []
    for n in range(steps):
        size //= 2
        copies = []
        for k in range(2):
            axis, bit = orders[k][n]
            keep = ((me_s if axis == "state" else me_o) // bit) % 2 * size
            where = {axis: partner(axis, bit)}
            give = pl.multiple_of(bases[k] + size - keep, 8)
            copies.append(remote(
                acc.at[pl.ds(give, size)], acc_got.at[pl.ds(spots[k], size)],
                acc_send.at[k, n], acc_recv.at[k, n], where,
            ))
            bases[k] = pl.multiple_of(bases[k] + keep, 8)
            trail.append((k, n, where, bases[k], size))
            if k == 0:
                copies.append(remote(rhs_sum, rhs_got.at[n], rhs_send.at[n], rhs_recv.at[n], where))
        for copy in copies:
            copy.start()
        for copy in copies:
            copy.wait()
        for k in range(2):
            acc[pl.ds(bases[k], size), :] += acc_got[spots[k] : spots[k] + size, :]
            spots[k] += size
        rhs_sum[...] += rhs_got[n]
    for k in range(2):
        full[pl.ds(bases[k], size), :] = acc[pl.ds(bases[k], size), :]
    for n in reversed(range(steps)):
        copies = [
            remote(
                full.at[pl.ds(base, size)], full.at[pl.ds(base, size)],
                acc_send.at[k, steps + n], acc_recv.at[k, steps + n], where,
            )
            for k, m, where, base, size in trail if m == n
        ]
        for copy in copies:
            copy.start()
        for copy in copies:
            copy.wait()

    for t in range(obs_n - 1):
        @pl.when((me_o < obs_n - 1) & (me_o - t >= 0))
        def _():
            for c in hop(clip(me_o - t), right_send, right_recv, t, clip(me_o + 1)):
                c.wait_send()

        @pl.when((me_o > 0) & (me_o + t <= obs_n - 1))
        def _():
            for c in hop(clip(me_o + t), left_send, left_recv, t, clip(me_o - 1)):
                c.wait_send()
    for t in range(len(state_bits)):
        for i in range(nb >> (t + 1)):
            part_copy(t, i).wait_send()
    out_ref[0 : full.shape[0], :] = full[...]
    out_ref[full.shape[0] :, :] = rhs_sum[...]


def observe(obs_n, state_n, ids, counts, cells, mean_row, ops, readings, stds):
    nb = ops.shape[0]
    members = cells.shape[1]
    rows = packed_rows(members, obs_n * state_n)
    rounds = len(bits_of(state_n))
    steps = len(bits_of(obs_n)) + rounds
    hops = pltpu.SemaphoreType.DMA((2, obs_n - 1))
    dma = lambda *shape: pltpu.SemaphoreType.DMA(shape)
    return pl.pallas_call(
        functools.partial(observe_kernel, obs_n, state_n),
        out_shape=jax.ShapeDtypeStruct((rows + 8, BLK), jnp.float32),
        in_specs=[pl.BlockSpec(memory_space=pltpu.SMEM)] * 2
        + [pl.BlockSpec(memory_space=pl.ANY)] * 5,
        out_specs=pl.BlockSpec(memory_space=pltpu.VMEM),
        scratch_shapes=[
            pltpu.VMEM(mean_row.shape, jnp.float32),
            pltpu.VMEM(ops.shape, jnp.bfloat16),
            pltpu.VMEM((nb, BLK), jnp.float32),
            pltpu.VMEM((nb, BLK), jnp.float32),
            dma(5),
            pltpu.VMEM((obs_n, BLK, members), jnp.bfloat16),
            pltpu.VMEM((obs_n, 16, BLK), jnp.bfloat16),
            pltpu.VMEM((nb // state_n, BLK, members), jnp.float32),
            pltpu.VMEM((nb, BLK, members), jnp.bfloat16),
            pltpu.VMEM((nb, BLK, members), jnp.bfloat16),
            pltpu.VMEM((nb, BLK), jnp.float32),
            pltpu.VMEM((rounds, nb, BLK), jnp.float32),
            pltpu.VMEM((rows, BLK), jnp.float32),
            pltpu.VMEM((rows, BLK), jnp.float32),
            pltpu.VMEM((rows, BLK), jnp.float32),
            pltpu.VMEM((8, BLK), jnp.float32),
            pltpu.VMEM((steps, 8, BLK), jnp.float32),
            hops, hops, hops, hops,
            dma(nb), dma(nb), dma(rounds), dma(rounds),
            dma(2, 2 * steps), dma(2, 2 * steps), dma(steps), dma(steps),
        ],
        compiler_params=pltpu.CompilerParams(
            collective_id=0, has_side_effects=True, vmem_limit_bytes=60 << 20
        ),
    )(ids, counts, cells, mean_row, ops, readings, stds)


def local(
    obs_n,
    state_n,
    anomalies,
    prior_ensemble_mean,
    operator_blocks,
    block_column_ids,
    observation_counts,
    observed_readings,
    observation_error_std,
):
    cells = anomalies[0]
    packed = observe(
        obs_n, state_n, block_column_ids[:, 0], observation_counts, cells, prior_ensemble_mean,
        operator_blocks[:, 0], observed_readings, observation_error_std,
    )
    return finish(packed, cells, prior_ensemble_mean)[None]


def solution(mesh):
    placed = (
        P("state", "obs", None),
        P("state", "obs"),
        P(("net", "obs"), "state", None, None, None),
        P(("net", "obs"), "state", None),
        P(("net", "obs")),
        P(("net", "obs"), None),
        P(("net", "obs"), None),
    )
    return jax.shard_map(
        functools.partial(local, mesh.shape["obs"], mesh.shape["state"]),
        mesh=mesh,
        in_specs=placed,
        out_specs=P(("net", "state"), "obs", None),
        check_vma=False,
    )
```

```python
import functools
import jax
import jax.numpy as jnp
from jax import lax
from jax.experimental import pallas as pl
from jax.experimental.pallas import tpu as pltpu
from jax.sharding import PartitionSpec as P

BLK = 128
HI = lax.Precision.HIGHEST
NT = (((1,), (1,)), ((), ()))


def inverse_factor(block, width=32):
    row = lax.broadcasted_iota(jnp.int32, (BLK, BLK), 0)
    col = lax.broadcasted_iota(jnp.int32, (BLK, BLK), 1)
    eye = (row == col).astype(jnp.float32)
    groups = BLK // 8
    left = [block[8 * g : 8 * g + 8] for g in range(groups)]
    right = [eye[8 * g : 8 * g + 8] for g in range(groups)]
    sub = lax.broadcasted_iota(jnp.int32, (8, 1), 0)
    lane = lax.broadcasted_iota(jnp.int32, (1, BLK), 1)
    local = width // 8
    for start in range(0, BLK, width):
        g0 = start // 8
        spread = [
            [jnp.broadcast_to(left[g0 + h][:, start + j : start + j + 1], (8, BLK)) for h in range(local)]
            for j in range(width)
        ]
        scaled = []
        roots = []
        for j in range(width):
            gj, ij = divmod(j, 8)
            pivot = spread[j][gj][ij : ij + 1]
            inv = 1.0 / pivot
            lrow = left[g0 + gj][ij : ij + 1] * inv
            rrow = right[g0 + gj][ij : ij + 1] * inv
            scaled.append(lrow)
            roots.append(lax.rsqrt(pivot))
            shared = [None if t <= j else spread[t][gj][ij : ij + 1] * inv for t in range(width)]
            for h in range(gj, local):
                m = spread[j][h]
                if h == gj:
                    if ij == 7:
                        continue
                    m = jnp.where(sub > ij, m, 0.0)
                for t in range(j + 1, width):
                    spread[t][h] = spread[t][h] - m * shared[t]
                left[g0 + h] = left[g0 + h] - m * lrow
                right[g0 + h] = right[g0 + h] - m * rrow
        upper_l = jnp.concatenate(left[g0 : g0 + local], axis=0)
        upper_r = jnp.concatenate(right[g0 : g0 + local], axis=0)
        end = start + width
        if end < BLK:
            low = jnp.where(lane >= end, jnp.concatenate(scaled, axis=0), 0.0)
            change = lax.dot_general(
                low, jnp.concatenate([upper_l, upper_r], axis=1), (((0,), (0,)), ((), ())),
                precision=HI, preferred_element_type=jnp.float32,
            )
            for h in range(end // 8, groups):
                left[h] = left[h] - change[8 * h : 8 * h + 8, :BLK]
                right[h] = right[h] - change[8 * h : 8 * h + 8, BLK:]
        scale = jnp.concatenate(roots, axis=0)
        for h in range(local):
            right[g0 + h] = right[g0 + h] * scale[8 * h : 8 * h + 8]
    return jnp.concatenate(right, axis=0)


def finish_kernel(packed_ref, anom_ref, mean_ref, out_ref, work):
    cells, members = anom_ref.shape
    total = members + cells + 8
    row = lax.broadcasted_iota(jnp.int32, (BLK, BLK), 0)
    col = lax.broadcasted_iota(jnp.int32, (BLK, BLK), 1)
    ridge = jnp.where(row == col, members - 1.0, 0.0)
    start = 0
    last = packed_ref.shape[0] - 8
    for j in range(members // BLK):
        size = members - j * BLK
        cols = slice(j * BLK, (j + 1) * BLK)
        if j:
            work[0 : j * BLK, cols] = jnp.zeros((j * BLK, BLK), jnp.float32)
        work[cols, cols] = packed_ref[start : start + BLK, :] + ridge
        if size > BLK:
            work[(j + 1) * BLK : members, cols] = packed_ref[start + BLK : start + size, :]
        start += size
    for j in range(members // BLK):
        cols = slice(j * BLK, (j + 1) * BLK)
        work[members + cells : total, cols] = jnp.broadcast_to(
            packed_ref[last + j : last + j + 1, :], (8, BLK)
        )
    work[members : members + cells, :] = anom_ref[...].astype(jnp.float32)

    for off in range(0, members, BLK):
        end = off + BLK
        inv = inverse_factor(work[off:end, off:end])
        x = lax.dot_general(
            work[end:total, off:end], inv, NT, precision=HI, preferred_element_type=jnp.float32
        )
        work[members:total, off:end] = x[members - end :]
        if end < members:
            work[end : end + BLK, end : end + BLK] -= lax.dot_general(
                x[:BLK], x[:BLK], NT, precision=HI, preferred_element_type=jnp.float32
            )
            work[end + BLK : total, end : end + BLK] -= lax.dot_general(
                x[BLK:], x[:BLK], NT, precision=HI, preferred_element_type=jnp.float32
            )
        for at in range(end + BLK, members, BLK):
            work[at:total, at : at + BLK] -= lax.dot_general(
                x[at - end :], x[at - end : at - end + BLK], NT, precision=HI,
                preferred_element_type=jnp.float32,
            )

    solved = work[members : members + cells, :]
    shift = jnp.sum(solved * work[members + cells : members + cells + 1, :], axis=1, keepdims=True)
    root = (members - 1.0) ** 0.5
    mean = jnp.broadcast_to(mean_ref[...], (BLK, cells)).T[:, 0:1]
    out_ref[...] = (mean + (root * solved + shift)).astype(jnp.bfloat16)


def finish(packed, cells, mean_row):
    ncells, members = cells.shape
    return pl.pallas_call(
        finish_kernel,
        out_shape=jax.ShapeDtypeStruct((ncells, members), jnp.bfloat16),
        in_specs=[pl.BlockSpec(memory_space=pltpu.VMEM)] * 3,
        out_specs=pl.BlockSpec(memory_space=pltpu.VMEM),
        scratch_shapes=[pltpu.VMEM((members + ncells + 8, members), jnp.float32)],
        compiler_params=pltpu.CompilerParams(vmem_limit_bytes=32 << 20),
    )(packed, cells, mean_row)


def packed_rows(members, ways):
    need = sum(members - j * BLK for j in range(members // BLK))
    step = 16 * ways
    return (need + step - 1) // step * step


def bits_of(n):
    return [1 << t for t in range(n.bit_length() - 1)]


def observe_kernel(
    obs_n, state_n, ids_ref, counts_ref, cells_hbm, mean_hbm, ops_hbm, read_hbm, std_hbm, out_ref,
    mean_row, ops_ref, read_ref, std_ref, load_sem,
    slab, slab_mean, part, sent, got, inno, inno_got, acc, acc_got, full, rhs_sum, rhs_got,
    right_send, right_recv, left_send, left_recv, part_send, part_recv, inno_send, inno_recv,
    acc_send, acc_recv, rhs_send, rhs_recv,
):
    me_o, me_s = lax.axis_index("obs"), lax.axis_index("state")
    nb, slots = ops_ref.shape[0], ops_ref.shape[1]
    members = slab.shape[2]
    state_bits, obs_bits = bits_of(state_n), bits_of(obs_n)

    loads = [
        pltpu.make_async_copy(src, dst, load_sem.at[n])
        for n, (src, dst) in enumerate([
            (cells_hbm, slab.at[me_o]), (mean_hbm, mean_row), (read_hbm, read_ref),
            (std_hbm, std_ref), (ops_hbm, ops_ref),
        ])
    ]
    for load in loads:
        load.start()

    def partner(axis, bit):
        me = me_s if axis == "state" else me_o
        return me + bit - 2 * bit * ((me // bit) % 2)

    barrier = pltpu.get_barrier_semaphore()
    greeted = [{"obs": lax.rem(me_o + 1, obs_n)}, {"obs": lax.rem(me_o + obs_n - 1, obs_n)}]
    greeted += [{"obs": partner("obs", b)} for b in obs_bits]
    greeted += [{"state": partner("state", b)} for b in state_bits]
    for where in greeted:
        pl.semaphore_signal(barrier, inc=1, device_id=where, device_id_type=pl.DeviceIdType.MESH)
    loads[0].wait()
    loads[1].wait()
    slab_mean[me_o] = jnp.broadcast_to(mean_row[...], (16, BLK)).astype(jnp.bfloat16)
    pl.semaphore_wait(barrier, len(greeted))

    def remote(src, dst, send, recv, where):
        return pltpu.make_async_remote_copy(
            src_ref=src, dst_ref=dst, send_sem=send, recv_sem=recv,
            device_id=where, device_id_type=pl.DeviceIdType.MESH,
        )

    def hop(block, sends, recvs, t, to):
        return [
            remote(slab.at[block], slab.at[block], sends.at[0, t], recvs.at[0, t], {"obs": to}),
            remote(slab_mean.at[block], slab_mean.at[block], sends.at[1, t], recvs.at[1, t], {"obs": to}),
        ]

    def clip(x):
        return jnp.clip(x, 0, obs_n - 1)

    for t in range(obs_n - 1):
        @pl.when((me_o < obs_n - 1) & (me_o - t >= 0))
        def _():
            for c in hop(clip(me_o - t), right_send, right_recv, t, clip(me_o + 1)):
                c.start()

        @pl.when((me_o > 0) & (me_o + t <= obs_n - 1))
        def _():
            for c in hop(clip(me_o + t), left_send, left_recv, t, clip(me_o - 1)):
                c.start()

        @pl.when(me_o - 1 - t >= 0)
        def _():
            for c in hop(clip(me_o - 1 - t), right_send, right_recv, t, clip(me_o - 1)):
                c.wait_recv()

        @pl.when(me_o + 1 + t <= obs_n - 1)
        def _():
            for c in hop(clip(me_o + 1 + t), left_send, left_recv, t, clip(me_o + 1)):
                c.wait_recv()

    for load in loads[2:]:
        load.wait()
    lane = lax.broadcasted_iota(jnp.int32, (1, BLK), 1)

    def weight_of(b):
        return jnp.where(lane < counts_ref[b], 1.0 / std_ref[pl.ds(b, 1), :], 0.0)

    @pl.loop(0, nb)
    def _(b):
        mean = jnp.zeros((16, BLK), jnp.float32)
        for j in range(slots):
            mean += lax.dot_general(
                slab_mean[ids_ref[b, j]], ops_ref[b, j], NT, preferred_element_type=jnp.float32
            )
        share = read_ref[pl.ds(b, 1), :] * (1.0 / state_n)
        inno[pl.ds(b, 1), :] = weight_of(b) * (share - mean[0:1])

    def inno_copy(t):
        where = {"state": partner("state", state_bits[t])}
        return remote(inno, inno_got.at[t], inno_send.at[t], inno_recv.at[t], where)

    inno_copy(0).start()

    def observe(b):
        rows = jnp.zeros((BLK, members), jnp.float32)
        for j in range(slots):
            rows += jnp.dot(ops_ref[b, j], slab[ids_ref[b, j]], preferred_element_type=jnp.float32)
        return rows * jnp.broadcast_to(weight_of(b), (BLK, BLK)).T[:, 0:1]

    def part_copy(t, i):
        n = nb - (nb >> t) + i
        where = {"state": partner("state", state_bits[t])}
        return remote(sent.at[n], got.at[n], part_send.at[n], part_recv.at[n], where)

    lows = [0]
    for t, bit in enumerate(state_bits):
        half = nb >> (t + 1)
        keep = (me_s // bit) % 2 * half
        give = lows[-1] + half - keep
        lows.append(lows[-1] + keep)

        def total(b, upto):
            value = observe(b)
            for u in range(upto):
                part_copy(u, b - lows[u + 1]).wait_recv()
                value += got[nb - (nb >> u) + b - lows[u + 1]].astype(jnp.float32)
            return value

        @pl.loop(0, half)
        def _(i):
            sent[nb - (nb >> t) + i] = total(give + i, t).astype(jnp.bfloat16)
            part_copy(t, i).start()

        inno_copy(t).wait()
        inno[...] += inno_got[t]
        if t + 1 < len(state_bits):
            inno_copy(t + 1).start()
    own = nb // state_n
    low = lows[-1]
    last = len(state_bits) - 1

    @pl.loop(0, own)
    def _(i):
        value = observe(low + i)
        for u in range(last):
            part_copy(u, low + i - lows[u + 1]).wait_recv()
            value += got[nb - (nb >> u) + low + i - lows[u + 1]].astype(jnp.float32)
        part[i] = value

    @pl.loop(0, own)
    def _(i):
        part_copy(last, i).wait_recv()
        part[i] += got[nb - (nb >> last) + i].astype(jnp.float32)

    scaled = part[...].reshape(own * BLK, members)
    row = 0
    for j in range(members // BLK):
        size = members - j * BLK
        acc[row : row + size, :] = lax.dot_general(
            scaled[:, j * BLK :], scaled[:, j * BLK : (j + 1) * BLK], (((0,), (0,)), ((), ())),
            precision=HI, preferred_element_type=jnp.float32,
        )
        row += size
    if row < acc.shape[0]:
        acc[row:, :] = jnp.zeros((acc.shape[0] - row, BLK), jnp.float32)
    rhs = jnp.zeros((8, members), jnp.float32)
    for i in range(own):
        rhs += jnp.dot(
            jnp.broadcast_to(inno[pl.ds(low + i, 1), :], (8, BLK)), scaled[i * BLK : (i + 1) * BLK],
            precision=HI, preferred_element_type=jnp.float32,
        )
    rhs_sum[...] = jnp.zeros((8, BLK), jnp.float32)
    for j in range(members // BLK):
        rhs_sum[j : j + 1, :] = rhs[0:1, j * BLK : (j + 1) * BLK]

    by_state = [("state", b) for b in state_bits]
    by_obs = [("obs", b) for b in obs_bits]
    orders = [by_state + by_obs, by_state[:1] + by_obs + by_state[1:]]
    steps = len(orders[0])
    size = acc.shape[0] // 2
    bases = [0, size]
    spots = [0, size]
    trail = []
    for n in range(steps):
        size //= 2
        copies = []
        for k in range(2):
            axis, bit = orders[k][n]
            keep = ((me_s if axis == "state" else me_o) // bit) % 2 * size
            where = {axis: partner(axis, bit)}
            give = pl.multiple_of(bases[k] + size - keep, 8)
            copies.append(remote(
                acc.at[pl.ds(give, size)], acc_got.at[pl.ds(spots[k], size)],
                acc_send.at[k, n], acc_recv.at[k, n], where,
            ))
            bases[k] = pl.multiple_of(bases[k] + keep, 8)
            trail.append((k, n, where, bases[k], size))
            if k == 0:
                copies.append(remote(rhs_sum, rhs_got.at[n], rhs_send.at[n], rhs_recv.at[n], where))
        for copy in copies:
            copy.start()
        for copy in copies:
            copy.wait()
        for k in range(2):
            acc[pl.ds(bases[k], size), :] += acc_got[spots[k] : spots[k] + size, :]
            spots[k] += size
        rhs_sum[...] += rhs_got[n]
    for k in range(2):
        full[pl.ds(bases[k], size), :] = acc[pl.ds(bases[k], size), :]
    for n in reversed(range(steps)):
        copies = [
            remote(
                full.at[pl.ds(base, size)], full.at[pl.ds(base, size)],
                acc_send.at[k, steps + n], acc_recv.at[k, steps + n], where,
            )
            for k, m, where, base, size in trail if m == n
        ]
        for copy in copies:
            copy.start()
        for copy in copies:
            copy.wait()

    for t in range(obs_n - 1):
        @pl.when((me_o < obs_n - 1) & (me_o - t >= 0))
        def _():
            for c in hop(clip(me_o - t), right_send, right_recv, t, clip(me_o + 1)):
                c.wait_send()

        @pl.when((me_o > 0) & (me_o + t <= obs_n - 1))
        def _():
            for c in hop(clip(me_o + t), left_send, left_recv, t, clip(me_o - 1)):
                c.wait_send()
    for t in range(len(state_bits)):
        for i in range(nb >> (t + 1)):
            part_copy(t, i).wait_send()
    out_ref[0 : full.shape[0], :] = full[...]
    out_ref[full.shape[0] :, :] = rhs_sum[...]


def observe(obs_n, state_n, ids, counts, cells, mean_row, ops, readings, stds):
    nb = ops.shape[0]
    members = cells.shape[1]
    rows = packed_rows(members, obs_n * state_n)
    rounds = len(bits_of(state_n))
    steps = len(bits_of(obs_n)) + rounds
    hops = pltpu.SemaphoreType.DMA((2, obs_n - 1))
    dma = lambda *shape: pltpu.SemaphoreType.DMA(shape)
    return pl.pallas_call(
        functools.partial(observe_kernel, obs_n, state_n),
        out_shape=jax.ShapeDtypeStruct((rows + 8, BLK), jnp.float32),
        in_specs=[pl.BlockSpec(memory_space=pltpu.SMEM)] * 2
        + [pl.BlockSpec(memory_space=pl.ANY)] * 5,
        out_specs=pl.BlockSpec(memory_space=pltpu.VMEM),
        scratch_shapes=[
            pltpu.VMEM(mean_row.shape, jnp.float32),
            pltpu.VMEM(ops.shape, jnp.bfloat16),
            pltpu.VMEM((nb, BLK), jnp.float32),
            pltpu.VMEM((nb, BLK), jnp.float32),
            dma(5),
            pltpu.VMEM((obs_n, BLK, members), jnp.bfloat16),
            pltpu.VMEM((obs_n, 16, BLK), jnp.bfloat16),
            pltpu.VMEM((nb // state_n, BLK, members), jnp.float32),
            pltpu.VMEM((nb, BLK, members), jnp.bfloat16),
            pltpu.VMEM((nb, BLK, members), jnp.bfloat16),
            pltpu.VMEM((nb, BLK), jnp.float32),
            pltpu.VMEM((rounds, nb, BLK), jnp.float32),
            pltpu.VMEM((rows, BLK), jnp.float32),
            pltpu.VMEM((rows, BLK), jnp.float32),
            pltpu.VMEM((rows, BLK), jnp.float32),
            pltpu.VMEM((8, BLK), jnp.float32),
            pltpu.VMEM((steps, 8, BLK), jnp.float32),
            hops, hops, hops, hops,
            dma(nb), dma(nb), dma(rounds), dma(rounds),
            dma(2, 2 * steps), dma(2, 2 * steps), dma(steps), dma(steps),
        ],
        compiler_params=pltpu.CompilerParams(
            collective_id=0, has_side_effects=True, vmem_limit_bytes=60 << 20
        ),
    )(ids, counts, cells, mean_row, ops, readings, stds)


def local(
    obs_n,
    state_n,
    anomalies,
    prior_ensemble_mean,
    operator_blocks,
    block_column_ids,
    observation_counts,
    observed_readings,
    observation_error_std,
):
    cells = anomalies[0]
    packed = observe(
        obs_n, state_n, block_column_ids[:, 0], observation_counts, cells, prior_ensemble_mean,
        operator_blocks[:, 0], observed_readings, observation_error_std,
    )
    return finish(packed, cells, prior_ensemble_mean)[None]


def solution(mesh):
    placed = (
        P("state", "obs", None),
        P("state", "obs"),
        P(("net", "obs"), "state", None, None, None),
        P(("net", "obs"), "state", None),
        P(("net", "obs")),
        P(("net", "obs"), None),
        P(("net", "obs"), None),
    )
    return jax.shard_map(
        functools.partial(local, mesh.shape["obs"], mesh.shape["state"]),
        mesh=mesh,
        in_specs=placed,
        out_specs=P(("net", "state"), "obs", None),
        check_vma=False,
    )
```
